32 devices in a mesh: groups: 2 (over y), wide: 4 (over z), narrow: 2 (over x), sub: 2 (over core).
Axes of the slice: x: 2, y: 2, z: 4, core: 2. Of those that a mesh axis runs over, the one named last changes fastest.
Arguments:
- mode_shapes: bfloat16 [48, 1024, 1024], P(('groups', 'wide'), 'narrow'), parts along dimension 0, may hold values from -0.25 to 0.25
- amplitudes: bfloat16 [2048, 64], P('groups', 'sub'), parts along dimension 0, may hold values from -6 to 6
- self_resistance: float32 [48, 1024], P(('groups', 'wide'), 'narrow'), parts along dimension 0, may hold values from 0.2 to 2
- out_factor: bfloat16 [48, 2, 1024, 256], P(('groups', 'wide'), None, 'narrow'), parts along dimension 0, may hold values from -0.375 to 0.375
- in_factor: bfloat16 [48, 2, 1024, 256], P(('groups', 'wide'), None, 'narrow'), parts along dimension 0, may hold values from -0.1875 to 0.1875
- block_source: int32 [96, 1], P('groups'), parts along dimension 0, may hold values from 0 to 3; in each aligned block of 12 rows (0 to 11, 12 to 23, ...) at most 3 rows name the same one
- block_cluster: int32 [96], P('groups'), parts along dimension 0, may hold values from 0 to 5
- block_rank: int32 [96], P('groups'), parts along dimension 0, may hold values from 64 to 256
Outputs:
- patch_force: bfloat16 [48, 64, 1024], P(('groups', 'wide'), 'sub', 'narrow'), parts along dimension 0
- modal_load: float32 [2048, 64], P(('groups', 'wide', 'narrow'), 'sub'), parts along dimension 0
The draws below stay inside these ranges and needn't reach their ends.
There are 2 independent parts, one for each index of `groups`. The reference program is written for one: setup_inputs(seed, part) draws one part's arguments, and reference() takes and returns one part's arrays. A program takes and returns all parts, laid end to end along the dimension named above; each array names one. Nothing has to cross between parts.
Inputs may be any that keep to these rules, and one draw needn't show every extreme that they name: Among the 12 blocks of one wide index (rows of block_source in aligned runs of that length), at most 3 name the same wide index, and some wide index is named exactly 3 times.
All inputs are finite; a program needn't handle non-finite values.
Results may differ from the reference program's by a relative error of at most 0.0095.
Values may be sent and summed in bfloat16 or wider, within the bound.
A program may use at most 64 MiB of HBM per device.

```python
import math
import jax
import jax.numpy as jnp
import numpy as np
from jax import lax

M = 1024
LOADS = 64
S = 1024
RMAX = 256
K = 2
CW = 6
NCL = 24
NBLK = 48
CAP = 3
N_WIDE = 4


def set_ends(drawn, rng, low, top_value):
    longest = drawn.shape.index(max(drawn.shape))
    spots = []
    for shift in (0, 1):
        where = [jax.random.randint(jax.random.fold_in(rng, axis), (), 0, length) for axis, length in enumerate(drawn.shape)]
        where[longest] = (where[longest] + shift) % drawn.shape[longest]
        spots.append(tuple(where))
    return drawn.at[spots[0]].set(low).at[spots[1]].set(top_value)


def raised(result, key, source, target, parts, factor):
    def block_of(axis_at):
        return (jnp.arange(result.shape[axis_at]) // (result.shape[axis_at] // parts)).reshape((-1,) + (1,) * (result.ndim - 1 - axis_at))

    near = jax.random.permutation(key, parts)[block_of(target)]
    second = (block_of(target) + parts // 2) % parts
    return jnp.where((block_of(source) == near) | (block_of(source) == second), factor * result, result)


def steps_of(rng, shape, split, least, largest):
    gain = 1.0
    for axis_at, shards_of in split:
        heights = jax.random.uniform(jax.random.fold_in(jax.random.fold_in(rng, 6), axis_at), (shards_of,), jnp.float32, least / len(split), largest / len(split))
        gain = gain * jnp.repeat(jnp.exp(heights), shape[axis_at] // shards_of).reshape((-1,) + (1,) * (len(shape) - 1 - axis_at))
    return gain


def routed_block(rng, own, number, rows, amount, top, most, slope):
    ranking = jax.random.permutation(rng, amount)
    heavy_load, usual = load_shares(amount, rows * top, most, slope, True), load_shares(amount, rows * top, most, slope, False)
    places = jnp.arange(amount)

    def named(sizes, offset_by):
        used = int((sizes > 0).sum())
        fixed = max(1, used // 4)
        shifted = fixed + (places - fixed + offset_by * (used - fixed)) % max(1, amount - fixed)
        return jnp.zeros((amount,), jnp.int32).at[ranking[jnp.where(places < fixed, places, shifted)]].set(jnp.asarray(sizes, jnp.int32))

    sizes = jnp.where(number % 4 == 0, named(heavy_load, number // 4), named(usual, number - number // 4 - 1))
    mixed = jax.random.permutation(jax.random.fold_in(own, 3), amount)
    donor, sink = mixed[0:amount // 2 * 2:2], mixed[1:amount // 2 * 2:2]
    margin = jnp.minimum(sizes[donor] - 1, most - sizes[sink]) // 2
    margin = jnp.where((donor == ranking[0]) | (sink == ranking[0]) | (sizes[sink] == 0), 0, jnp.maximum(margin, 0))
    shifted = jax.random.randint(jax.random.fold_in(own, 4), (amount // 2,), 0, 1 << 20) % (margin + 1)
    sizes = sizes.at[donor].add(-shifted).at[sink].add(shifted)
    members = jnp.searchsorted(jnp.cumsum(sizes), jnp.arange(rows * top), side="right").astype(jnp.int32)
    table = members.reshape(top, rows).T
    table = table[jax.random.permutation(jax.random.fold_in(own, 1), rows)]
    offset_by = jax.random.randint(jax.random.fold_in(own, 2), (rows, 1), 0, top)
    return jnp.take_along_axis(table, (jnp.arange(top)[None, :] + offset_by) % top, axis=1)


def load_shares(amount, total, most, lean, full):
    loads = [(1 << 20) // math.isqrt(grade ** lean) + 1 for grade in range(1, amount + 1)]
    largest = most if full else min(most, max(-(-total // amount), total * loads[0] // sum(loads)))
    least = 1 if total - largest >= amount - 1 else 0
    given, spare = [largest] + [least] * (amount - 1), total - largest - least * (amount - 1)
    while spare > 0:
        candidates = [i for i in range(1, amount) if given[i] < largest] or [i for i in range(1, amount) if given[i] < most]
        pool, remaining = sum([loads[i] for i in candidates]), spare
        for i in candidates:
            more = min(most - given[i], max(1, remaining * loads[i] // pool), spare)
            given[i] = given[i] + more
            spare = spare - more
    return np.array(given)


def centred(stream_key, shape, scale, most, shards=(), held_as=jnp.bfloat16):
    gain = steps_of(stream_key, shape, shards, -0.22, 0.18) if shards else 1.0
    drawn = jax.random.normal(stream_key, shape, jnp.float32) * scale * gain
    return jnp.minimum(jnp.maximum(drawn, -most), most).astype(held_as)


def bell_draw_with(stream_key, shape, deviation, reach, cuts, heavy, kind=jnp.bfloat16):
    entries = deviation * jax.random.normal(stream_key, shape, jnp.float32)
    if cuts:
        entries = entries * steps_of(stream_key, shape, cuts, -0.22, 0.18)
    return jnp.clip(raised(entries, jax.random.fold_in(stream_key, 3), *heavy), -reach, reach).astype(kind)


def setup_inputs(seed: int = 0, part: int = 0) -> dict:
    seeds = jax.random.split(jax.random.key(seed), 9)
    own_keys = jax.random.split(jax.random.fold_in(seeds[8], part), 9)
    mode_shapes = bell_draw_with(own_keys[0], (NCL, S, M), M ** -0.5, 0.25, ((0, 4), (1, 2)), (0, 2, 4, 2.0))
    amplitudes = centred(own_keys[1], (M, LOADS), 1.0, 6.0, ((1, 2),))
    self_resistance = jnp.clip(jnp.exp(math.log(2.0) - 2.3025851 * jax.random.uniform(own_keys[2], (NCL, S), jnp.float32) ** steps_of(own_keys[2], (NCL, S), ((0, 4), (1, 2)), -0.2, 0.2)), 0.2, 2.0)
    out_factor = centred(own_keys[3], (NCL, K, S, RMAX), RMAX ** -0.5, 0.375, ((0, 4), (2, 2)))
    in_factor = centred(own_keys[4], (NCL, K, S, RMAX), S ** -0.5, 0.1875, ((0, 4), (2, 2)))
    block_source_keys = jax.random.split(jax.random.fold_in(own_keys[5], 1), NBLK // (CW * K))
    block_source_turns = jax.random.permutation(jax.random.fold_in(own_keys[5], 3), NBLK // (CW * K))
    block_source = jax.vmap(lambda own, number: routed_block(jax.random.fold_in(own_keys[5], 2), own, number, CW * K, N_WIDE, 1, CAP, 2))(block_source_keys, block_source_turns).reshape((NBLK, 1))
    block_cluster = set_ends(jax.random.randint(own_keys[6], (NBLK,), 0, CW), jax.random.fold_in(own_keys[6], 1), 0, CW - 1).astype(jnp.int32)
    block_rank = set_ends(jax.random.randint(own_keys[7], (NBLK,), RMAX // 4, RMAX + 1), jax.random.fold_in(own_keys[7], 1), RMAX // 4, RMAX).astype(jnp.int32)
    return dict(mode_shapes=mode_shapes, amplitudes=amplitudes, self_resistance=self_resistance, out_factor=out_factor, in_factor=in_factor, block_source=block_source, block_cluster=block_cluster, block_rank=block_rank)


def reference(mode_shapes, amplitudes, self_resistance, out_factor, in_factor, block_source, block_cluster, block_rank):
    flat_basis = mode_shapes.reshape(NCL * S, M)
    velocity = jnp.dot(flat_basis, amplitudes, preferred_element_type=jnp.float32)
    velocity = velocity.reshape(NCL, S, LOADS).transpose(0, 2, 1).astype(jnp.bfloat16)
    near_load = (self_resistance[:, None, :] * velocity.astype(jnp.float32)).astype(jnp.bfloat16)
    columns = (block_source[:, 0] * CW + block_cluster).astype(jnp.int32)
    pieces = jnp.take(velocity, columns, axis=0).astype(jnp.float32)
    rights = in_factor.reshape(NBLK, S, RMAX).astype(jnp.float32)
    summed = jnp.einsum('blp,bpr->blr', pieces, rights, precision=lax.Precision.HIGHEST)
    rank_mask = (jnp.arange(RMAX, dtype=jnp.int32)[None, :] < block_rank[:, None]).astype(jnp.float32)
    coeffs = (summed * rank_mask[:, None, :]).astype(jnp.bfloat16)
    left_blocks = out_factor.reshape(NBLK, S, RMAX).astype(jnp.float32)
    far_blocks = jnp.einsum('blr,bpr->blp', coeffs.astype(jnp.float32), left_blocks, precision=lax.Precision.HIGHEST)
    far_load = far_blocks.reshape(NCL, K, LOADS, S).sum(axis=1).astype(jnp.bfloat16)
    patch_force = (near_load.astype(jnp.float32) + far_load.astype(jnp.float32)).astype(jnp.bfloat16)
    force_rows = patch_force.transpose(0, 2, 1).reshape(NCL * S, LOADS)
    modal_load = jnp.dot(flat_basis.T, force_rows, preferred_element_type=jnp.float32)
    modal_load = modal_load * (M / (NCL * S)) ** 0.5
    return patch_force, modal_load
```

```python
import functools

import jax
import jax.numpy as jnp
from jax import lax
from jax.experimental import pallas as pl
from jax.experimental.pallas import tpu as pltpu
from jax.sharding import PartitionSpec as P

MESH = pl.DeviceIdType.MESH
NT = (((1,), (1,)), ((), ()))


def partner(position, step, count):
    result, bit = 0, 1
    while bit < count:
        digit = lax.rem(lax.div(position, bit), 2)
        result = result + bit * ((1 - digit) if step & bit else digit)
        bit *= 2
    return result


def slots_of(source_ref, start, per_wide, wanted, cap):
    count = jnp.int32(0)
    rows = [jnp.int32(0)] * cap
    matches, counts = [], []
    for row in range(per_wide):
        hit = source_ref[start + row] == wanted
        for slot in range(cap):
            rows[slot] = jnp.where(hit & (count == slot), row, rows[slot])
        matches.append(hit)
        counts.append(jnp.minimum(count, cap - 1))
        count = count + jnp.where(hit, 1, 0)
    return rows, matches, counts


def kernel(
    wide_count, narrow_count, cap, split, dense, scale,
    source_ref, cluster_ref, rank_ref, amp_ref, res_ref, mode_hbm, in_hbm, out_hbm,
    force_hbm, modal_ref,
    mode_v, in_v, out_v, vel, near, force, outgoing, incoming, part_own, part_send, part_recv,
    coeffs, load_send, load_own, load_recv,
    mode_sem, in_sem, out_sem, force_sem, vel_send_sem, vel_recv_sem, part_send_sem, part_recv_sem,
    load_send_sem, load_recv_sem,
):
    wide, narrow = lax.axis_index("wide"), lax.axis_index("narrow")
    clusters, piece_rows, modes = mode_v.shape
    per_wide = in_v.shape[0]
    loads = vel.shape[1]
    rank_width = in_v.shape[2]
    group = cap // split

    mode_copies = [
        pltpu.make_async_copy(mode_hbm.at[c], mode_v.at[c], mode_sem.at[c]) for c in range(clusters)
    ]
    for copy in mode_copies:
        copy.start()
    in_copy = pltpu.make_async_copy(in_hbm, in_v, in_sem)
    in_copy.start()
    out_copy = pltpu.make_async_copy(out_hbm, out_v, out_sem)
    out_copy.start()

    wides = [partner(wide, step, wide_count) for step in range(wide_count)]
    narrows = [partner(narrow, step, narrow_count) for step in range(narrow_count)]
    barrier = pltpu.get_barrier_semaphore()
    for dw in range(wide_count):
        for dn in range(narrow_count):
            if dw or dn:
                pl.semaphore_signal(
                    barrier, inc=1, device_id={"wide": wides[dw], "narrow": narrows[dn]}, device_id_type=MESH
                )

    amps = amp_ref[...]
    own_start = wide * per_wide
    block_rows, slot_table = [], [jnp.int32(0)] * per_wide
    for dw in range(wide_count):
        rows, matches, counts = slots_of(source_ref, own_start, per_wide, wides[dw], cap)
        block_rows.append(rows)
        for row in range(per_wide):
            slot_table[row] = jnp.where(matches[row], dw * cap + counts[row], slot_table[row])
    wanted = []
    for dw in range(wide_count):
        rows, _, _ = slots_of(source_ref, wides[dw] * per_wide, per_wide, wide, cap)
        wanted.append([cluster_ref[wides[dw] * per_wide + row] for row in rows])

    for c in range(clusters):
        mode_copies[c].wait()
        vel[c] = lax.dot_general(amps, mode_v[c], NT, preferred_element_type=jnp.float32).astype(jnp.bfloat16)

    pl.semaphore_wait(barrier, wide_count * narrow_count - 1)

    def vel_copy(dw, slot):
        return pltpu.make_async_remote_copy(
            src_ref=outgoing.at[dw, slot],
            dst_ref=incoming.at[dw, slot],
            send_sem=vel_send_sem.at[dw, slot],
            recv_sem=vel_recv_sem.at[dw, slot],
            device_id={"wide": wides[dw]},
            device_id_type=MESH,
        )

    def part_copy(dw, piece, dn):
        span = pl.ds(piece * group, group)
        return pltpu.make_async_remote_copy(
            src_ref=part_send.at[dw, span],
            dst_ref=part_recv.at[dn, dw, span],
            send_sem=part_send_sem.at[dn, dw, piece],
            recv_sem=part_recv_sem.at[dn, dw, piece],
            device_id={"narrow": narrows[dn]},
            device_id_type=MESH,
        )

    def load_copy(dw, dn):
        return pltpu.make_async_remote_copy(
            src_ref=load_send.at[dw, narrows[dn]],
            dst_ref=load_recv.at[dw, dn],
            send_sem=load_send_sem.at[dw, dn],
            recv_sem=load_recv_sem.at[dw, dn],
            device_id={"wide": wides[dw], "narrow": narrows[dn]},
            device_id_type=MESH,
        )

    for dw in range(1, wide_count):
        for slot in range(cap):
            outgoing[dw, slot] = vel[wanted[dw][slot]]
            vel_copy(dw, slot).start()

    in_copy.wait()
    for dw in range(wide_count):
        for piece in range(split):
            for slot in range(piece * group, (piece + 1) * group):
                if dw:
                    vel_copy(dw, slot).wait_recv()
                    value = incoming[dw, slot]
                else:
                    value = vel[wanted[0][slot]]
                product = jnp.dot(value, in_v[block_rows[dw][slot]], preferred_element_type=jnp.float32)
                part_own[dw, slot] = product
                part_send[dw, slot] = product.astype(jnp.bfloat16)
            for dn in range(1, narrow_count):
                part_copy(dw, piece, dn).start()
        if dw == 0:
            for c in range(clusters):
                near[c] = (res_ref[pl.ds(c, 1), :] * vel[c].astype(jnp.float32)).astype(jnp.bfloat16)

    lanes = lax.broadcasted_iota(jnp.int32, (loads, rank_width), 1)
    for dw in range(wide_count):
        for piece in range(split):
            for dn in range(1, narrow_count):
                part_copy(dw, piece, dn).wait_recv()
            for slot in range(piece * group, (piece + 1) * group):
                total = part_own[dw, slot]
                for dn in range(1, narrow_count):
                    total = total + part_recv[dn, dw, slot].astype(jnp.float32)
                rank = rank_ref[own_start + block_rows[dw][slot]]
                coeffs[dw * cap + slot] = jnp.where(lanes < rank, total, 0.0).astype(jnp.bfloat16)

    out_copy.wait()
    blocks_per = per_wide // clusters
    for c in range(clusters):
        far = jnp.zeros((loads, piece_rows), jnp.float32)
        for k in range(blocks_per):
            row = c * blocks_per + k
            far = far + lax.dot_general(
                coeffs[slot_table[row]], out_v[row], NT, preferred_element_type=jnp.float32
            )
        far = far.astype(jnp.bfloat16).astype(jnp.float32)
        force[c] = (near[c].astype(jnp.float32) + far).astype(jnp.bfloat16)
    force_copy = pltpu.make_async_copy(force, force_hbm, force_sem)
    force_copy.start()

    order = list(range(1, wide_count))[::-1] + [0]
    if dense:
        columns = modes // wide_count
        rows = columns // narrow_count
        for dw in order:
            span = pl.ds(pl.multiple_of(wides[dw] * columns, 128), columns)
            total = jnp.zeros((loads, columns), jnp.float32)
            for c in range(clusters):
                total = total + jnp.dot(force[c], mode_v[c, :, span], preferred_element_type=jnp.float32)
            total = total * scale
            for n in range(narrow_count):
                piece = total[:, n * rows : (n + 1) * rows]
                load_send[dw, n] = piece.astype(load_send.dtype)
                if dw == 0:
                    load_own[n] = piece
            for dn in range(narrow_count):
                if dw or dn:
                    load_copy(dw, dn).start()
        result = load_own[narrow]
    else:
        total = jnp.zeros((loads, modes), jnp.float32)
        for c in range(clusters):
            total = total + jnp.dot(force[c], mode_v[c], preferred_element_type=jnp.float32)
        rows = modes // (wide_count * narrow_count)
        total = (total * scale).T.reshape(wide_count, narrow_count, rows, loads)
        for w in range(wide_count):
            load_own[w] = total[w]
        for dw in order:
            load_send[dw] = load_own[wides[dw]]
            for dn in range(narrow_count):
                if dw or dn:
                    load_copy(dw, dn).start()
        result = load_own[wide, narrow]
    for dw in order:
        for dn in range(narrow_count):
            if dw or dn:
                load_copy(dw, dn).wait_recv()
                result = result + load_recv[dw, dn].astype(jnp.float32)
    modal_ref[...] = result if dense else result.T

    force_copy.wait()
    for dw in range(wide_count):
        if dw:
            for slot in range(cap):
                vel_copy(dw, slot).wait_send()
        for dn in range(narrow_count):
            if dn:
                for piece in range(split):
                    part_copy(dw, piece, dn).wait_send()
            if dw or dn:
                load_copy(dw, dn).wait_send()


def per_device(
    mode_shapes,
    amplitudes,
    self_resistance,
    out_factor,
    in_factor,
    block_source,
    block_cluster,
    block_rank,
):
    clusters, piece_rows, modes = mode_shapes.shape
    loads = amplitudes.shape[1]
    blocks_per, rank_width = out_factor.shape[1], out_factor.shape[3]
    wide_count = lax.axis_size("wide")
    narrow_count = lax.axis_size("narrow")
    per_wide = clusters * blocks_per
    cap = min(per_wide, max(2, -(-per_wide // wide_count)))
    split = cap if wide_count <= 4 else 1
    rows = modes // (wide_count * narrow_count)
    dense = rows % 128 == 0
    scale = (modes / (wide_count * narrow_count * clusters * piece_rows)) ** 0.5
    bf16, f32 = jnp.bfloat16, jnp.float32
    if dense:
        load_shapes = [
            pltpu.VMEM((wide_count, narrow_count, loads, rows), bf16),
            pltpu.VMEM((narrow_count, loads, rows), f32),
            pltpu.VMEM((wide_count, narrow_count, loads, rows), bf16),
        ]
    else:
        load_shapes = [pltpu.VMEM((wide_count, narrow_count, rows, loads), f32)] * 3
    smem = pl.BlockSpec(memory_space=pltpu.SMEM)
    vmem = pl.BlockSpec(memory_space=pltpu.VMEM)
    hbm = pl.BlockSpec(memory_space=pl.ANY)
    dma = pltpu.SemaphoreType.DMA
    force, modal = pl.pallas_call(
        functools.partial(kernel, wide_count, narrow_count, cap, split, dense, scale),
        out_shape=(
            jax.ShapeDtypeStruct((clusters, loads, piece_rows), bf16),
            jax.ShapeDtypeStruct((loads, rows), f32),
        ),
        in_specs=[smem, smem, smem, vmem, vmem, hbm, hbm, hbm],
        out_specs=(hbm, vmem),
        scratch_shapes=[
            pltpu.VMEM((clusters, piece_rows, modes), bf16),
            pltpu.VMEM((per_wide, piece_rows, rank_width), bf16),
            pltpu.VMEM((per_wide, piece_rows, rank_width), bf16),
            pltpu.VMEM((clusters, loads, piece_rows), bf16),
            pltpu.VMEM((clusters, loads, piece_rows), bf16),
            pltpu.VMEM((clusters, loads, piece_rows), bf16),
            pltpu.VMEM((wide_count, cap, loads, piece_rows), bf16),
            pltpu.VMEM((wide_count, cap, loads, piece_rows), bf16),
            pltpu.VMEM((wide_count, cap, loads, rank_width), f32),
            pltpu.VMEM((wide_count, cap, loads, rank_width), bf16),
            pltpu.VMEM((narrow_count, wide_count, cap, loads, rank_width), bf16),
            pltpu.VMEM((wide_count * cap, loads, rank_width), bf16),
            *load_shapes,
            dma((clusters,)),
            dma,
            dma,
            dma,
            dma((wide_count, cap)),
            dma((wide_count, cap)),
            dma((narrow_count, wide_count, split)),
            dma((narrow_count, wide_count, split)),
            dma((wide_count, narrow_count)),
            dma((wide_count, narrow_count)),
        ],
        compiler_params=pltpu.CompilerParams(
            collective_id=0, has_side_effects=True, vmem_limit_bytes=60 * 1024 * 1024
        ),
    )(
        block_source.reshape(-1),
        block_cluster,
        block_rank,
        amplitudes.T,
        self_resistance,
        mode_shapes,
        in_factor.reshape(per_wide, piece_rows, rank_width),
        out_factor.reshape(per_wide, piece_rows, rank_width),
    )
    return force, modal.T


def solution(mesh):
    return jax.shard_map(
        per_device,
        mesh=mesh,
        in_specs=(
            P(("groups", "wide"), "narrow", None),
            P("groups", "sub"),
            P(("groups", "wide"), "narrow"),
            P(("groups", "wide"), None, "narrow", None),
            P(("groups", "wide"), None, "narrow", None),
            P("groups", None),
            P("groups"),
            P("groups"),
        ),
        out_specs=(P(("groups", "wide"), "sub", "narrow"), P(("groups", "wide", "narrow"), "sub")),
        check_vma=False,
    )
```

```python
import functools

import jax
import jax.numpy as jnp
from jax import lax
from jax.experimental import pallas as pl
from jax.experimental.pallas import tpu as pltpu
from jax.sharding import PartitionSpec as P

MESH = pl.DeviceIdType.MESH
NT = (((1,), (1,)), ((), ()))


def partner(position, step, count):
    result, bit = 0, 1
    while bit < count:
        digit = lax.rem(lax.div(position, bit), 2)
        result = result + bit * ((1 - digit) if step & bit else digit)
        bit *= 2
    return result


def slots_of(source_ref, start, per_wide, wanted, cap):
    count = jnp.int32(0)
    rows = [jnp.int32(0)] * cap
    matches, counts = [], []
    for row in range(per_wide):
        hit = source_ref[start + row] == wanted
        for slot in range(cap):
            rows[slot] = jnp.where(hit & (count == slot), row, rows[slot])
        matches.append(hit)
        counts.append(jnp.minimum(count, cap - 1))
        count = count + jnp.where(hit, 1, 0)
    return rows, matches, counts


def kernel(
    wide_count, narrow_count, cap, split, dense, scale,
    source_hbm, cluster_hbm, rank_hbm, amp_hbm, res_hbm, mode_hbm, in_hbm, out_hbm,
    force, modal_ref,
    source_ref, cluster_ref, rank_ref, amp_ref, res_ref, mode_v, in_v, out_v, vel, near, outgoing, incoming, part_own, part_send, part_recv,
    coeffs, load_send, load_own, load_recv,
    table_sem, mode_sem, in_sem, out_sem, vel_send_sem, vel_recv_sem, part_send_sem, part_recv_sem,
    load_send_sem, load_recv_sem,
):
    wide, narrow = lax.axis_index("wide"), lax.axis_index("narrow")
    clusters, piece_rows, modes = mode_v.shape
    per_wide = in_v.shape[0]
    loads = vel.shape[1]
    rank_width = in_v.shape[2]
    group = cap // split

    wides = [partner(wide, step, wide_count) for step in range(wide_count)]
    narrows = [partner(narrow, step, narrow_count) for step in range(narrow_count)]
    barrier = pltpu.get_barrier_semaphore()
    for dw in range(wide_count):
        for dn in range(narrow_count):
            if dw or dn:
                pl.semaphore_signal(
                    barrier, inc=1, device_id={"wide": wides[dw], "narrow": narrows[dn]}, device_id_type=MESH
                )

    small_copies = [
        pltpu.make_async_copy(src, dst, table_sem.at[i])
        for i, (src, dst) in enumerate(
            (
                (source_hbm, source_ref),
                (cluster_hbm, cluster_ref),
                (amp_hbm, amp_ref),
                (rank_hbm, rank_ref),
                (res_hbm, res_ref),
            )
        )
    ]
    for copy in small_copies[:3]:
        copy.start()
    mode_copies = [
        pltpu.make_async_copy(mode_hbm.at[c], mode_v.at[c], mode_sem.at[c]) for c in range(clusters)
    ]
    for copy in mode_copies:
        copy.start()
    for copy in small_copies[3:]:
        copy.start()
    in_copy = pltpu.make_async_copy(in_hbm, in_v, in_sem)
    in_copy.start()
    out_copy = pltpu.make_async_copy(out_hbm, out_v, out_sem)
    out_copy.start()

    small_copies[0].wait()
    small_copies[1].wait()
    own_start = wide * per_wide
    block_rows, slot_table = [], [jnp.int32(0)] * per_wide
    for dw in range(wide_count):
        rows, matches, counts = slots_of(source_ref, own_start, per_wide, wides[dw], cap)
        block_rows.append(rows)
        for row in range(per_wide):
            slot_table[row] = jnp.where(matches[row], dw * cap + counts[row], slot_table[row])
    wanted = []
    for dw in range(wide_count):
        rows, _, _ = slots_of(source_ref, wides[dw] * per_wide, per_wide, wide, cap)
        wanted.append([cluster_ref[wides[dw] * per_wide + row] for row in rows])

    small_copies[2].wait()
    amps = amp_ref[...]
    for c in range(clusters):
        mode_copies[c].wait()
        vel[c] = lax.dot_general(amps, mode_v[c], NT, preferred_element_type=jnp.float32).astype(jnp.bfloat16)

    pl.semaphore_wait(barrier, wide_count * narrow_count - 1)

    def vel_copy(dw, slot):
        return pltpu.make_async_remote_copy(
            src_ref=outgoing.at[dw, slot],
            dst_ref=incoming.at[dw, slot],
            send_sem=vel_send_sem.at[dw, slot],
            recv_sem=vel_recv_sem.at[dw, slot],
            device_id={"wide": wides[dw]},
            device_id_type=MESH,
        )

    def part_copy(dw, piece, dn):
        span = pl.ds(piece * group, group)
        return pltpu.make_async_remote_copy(
            src_ref=part_send.at[dw, span],
            dst_ref=part_recv.at[dn, dw, span],
            send_sem=part_send_sem.at[dn, dw, piece],
            recv_sem=part_recv_sem.at[dn, dw, piece],
            device_id={"narrow": narrows[dn]},
            device_id_type=MESH,
        )

    def load_copy(dw, dn):
        return pltpu.make_async_remote_copy(
            src_ref=load_send.at[dw, narrows[dn]],
            dst_ref=load_recv.at[dw, dn],
            send_sem=load_send_sem.at[dw, dn],
            recv_sem=load_recv_sem.at[dw, dn],
            device_id={"wide": wides[dw], "narrow": narrows[dn]},
            device_id_type=MESH,
        )

    for dw in range(1, wide_count):
        for slot in range(cap):
            outgoing[dw, slot] = vel[wanted[dw][slot]]
            vel_copy(dw, slot).start()

    for copy in small_copies[3:]:
        copy.wait()
    in_copy.wait()
    for dw in range(wide_count):
        for piece in range(split):
            for slot in range(piece * group, (piece + 1) * group):
                if dw:
                    vel_copy(dw, slot).wait_recv()
                    value = incoming[dw, slot]
                else:
                    value = vel[wanted[0][slot]]
                product = jnp.dot(value, in_v[block_rows[dw][slot]], preferred_element_type=jnp.float32)
                part_own[dw, slot] = product
                part_send[dw, slot] = product.astype(jnp.bfloat16)
            for dn in range(1, narrow_count):
                part_copy(dw, piece, dn).start()
        if dw == 0:
            for c in range(clusters):
                near[c] = (res_ref[pl.ds(c, 1), :] * vel[c].astype(jnp.float32)).astype(jnp.bfloat16)

    lanes = lax.broadcasted_iota(jnp.int32, (loads, rank_width), 1)
    for dw in range(wide_count):
        for piece in range(split):
            for dn in range(1, narrow_count):
                part_copy(dw, piece, dn).wait_recv()
            for slot in range(piece * group, (piece + 1) * group):
                total = part_own[dw, slot]
                for dn in range(1, narrow_count):
                    total = total + part_recv[dn, dw, slot].astype(jnp.float32)
                rank = rank_ref[own_start + block_rows[dw][slot]]
                coeffs[dw * cap + slot] = jnp.where(lanes < rank, total, 0.0).astype(jnp.bfloat16)

    out_copy.wait()
    blocks_per = per_wide // clusters
    for c in range(clusters):
        far = jnp.zeros((loads, piece_rows), jnp.float32)
        for k in range(blocks_per):
            row = c * blocks_per + k
            far = far + lax.dot_general(
                coeffs[slot_table[row]], out_v[row], NT, preferred_element_type=jnp.float32
            )
        far = far.astype(jnp.bfloat16).astype(jnp.float32)
        force[c] = (near[c].astype(jnp.float32) + far).astype(jnp.bfloat16)

    order = list(range(1, wide_count))[::-1] + [0]
    if dense:
        columns = modes // wide_count
        rows = columns // narrow_count
        for dw in order:
            span = pl.ds(pl.multiple_of(wides[dw] * columns, 128), columns)
            total = jnp.zeros((loads, columns), jnp.float32)
            for c in range(clusters):
                total = total + jnp.dot(force[c], mode_v[c, :, span], preferred_element_type=jnp.float32)
            total = total * scale
            for n in range(narrow_count):
                piece = total[:, n * rows : (n + 1) * rows]
                load_send[dw, n] = piece.astype(load_send.dtype)
                if dw == 0:
                    load_own[n] = piece
            for dn in range(narrow_count):
                if dw or dn:
                    load_copy(dw, dn).start()
        result = load_own[narrow]
    else:
        total = jnp.zeros((loads, modes), jnp.float32)
        for c in range(clusters):
            total = total + jnp.dot(force[c], mode_v[c], preferred_element_type=jnp.float32)
        rows = modes // (wide_count * narrow_count)
        total = (total * scale).T.reshape(wide_count, narrow_count, rows, loads)
        for w in range(wide_count):
            load_own[w] = total[w]
        for dw in order:
            load_send[dw] = load_own[wides[dw]]
            for dn in range(narrow_count):
                if dw or dn:
                    load_copy(dw, dn).start()
        result = load_own[wide, narrow]
    for dw in order:
        for dn in range(narrow_count):
            if dw or dn:
                load_copy(dw, dn).wait_recv()
                result = result + load_recv[dw, dn].astype(jnp.float32)
    modal_ref[...] = result if dense else result.T

    for dw in range(wide_count):
        if dw:
            for slot in range(cap):
                vel_copy(dw, slot).wait_send()
        for dn in range(narrow_count):
            if dn:
                for piece in range(split):
                    part_copy(dw, piece, dn).wait_send()
            if dw or dn:
                load_copy(dw, dn).wait_send()


def finish(force_ref, modal_ref, force_out, modal_out):
    force_out[...] = force_ref[...]
    modal_out[...] = modal_ref[...]


def per_device(
    mode_shapes,
    amplitudes,
    self_resistance,
    out_factor,
    in_factor,
    block_source,
    block_cluster,
    block_rank,
):
    clusters, piece_rows, modes = mode_shapes.shape
    loads = amplitudes.shape[1]
    blocks_per, rank_width = out_factor.shape[1], out_factor.shape[3]
    wide_count = lax.axis_size("wide")
    narrow_count = lax.axis_size("narrow")
    per_wide = clusters * blocks_per
    cap = min(per_wide, max(2, -(-per_wide // wide_count)))
    split = cap if wide_count <= 4 else 1
    rows = modes // (wide_count * narrow_count)
    dense = rows % 128 == 0
    scale = (modes / (wide_count * narrow_count * clusters * piece_rows)) ** 0.5
    bf16, f32 = jnp.bfloat16, jnp.float32
    if dense:
        load_shapes = [
            pltpu.VMEM((wide_count, narrow_count, loads, rows), bf16),
            pltpu.VMEM((narrow_count, loads, rows), f32),
            pltpu.VMEM((wide_count, narrow_count, loads, rows), bf16),
        ]
    else:
        load_shapes = [pltpu.VMEM((wide_count, narrow_count, rows, loads), f32)] * 3
    vmem = pl.BlockSpec(memory_space=pltpu.VMEM)
    hbm = pl.BlockSpec(memory_space=pl.ANY)
    dma = pltpu.SemaphoreType.DMA
    force, modal = pl.pallas_call(
        functools.partial(kernel, wide_count, narrow_count, cap, split, dense, scale),
        out_shape=(
            jax.ShapeDtypeStruct((clusters, loads, piece_rows), bf16),
            jax.ShapeDtypeStruct((loads, rows), f32),
        ),
        in_specs=[hbm] * 8,
        out_specs=(vmem, vmem),
        scratch_shapes=[
            pltpu.SMEM(block_cluster.shape, jnp.int32),
            pltpu.SMEM(block_cluster.shape, jnp.int32),
            pltpu.SMEM(block_cluster.shape, jnp.int32),
            pltpu.VMEM((loads, modes), bf16),
            pltpu.VMEM((clusters, piece_rows), f32),
            pltpu.VMEM((clusters, piece_rows, modes), bf16),
            pltpu.VMEM((per_wide, piece_rows, rank_width), bf16),
            pltpu.VMEM((per_wide, piece_rows, rank_width), bf16),
            pltpu.VMEM((clusters, loads, piece_rows), bf16),
            pltpu.VMEM((clusters, loads, piece_rows), bf16),
            pltpu.VMEM((wide_count, cap, loads, piece_rows), bf16),
            pltpu.VMEM((wide_count, cap, loads, piece_rows), bf16),
            pltpu.VMEM((wide_count, cap, loads, rank_width), f32),
            pltpu.VMEM((wide_count, cap, loads, rank_width), bf16),
            pltpu.VMEM((narrow_count, wide_count, cap, loads, rank_width), bf16),
            pltpu.VMEM((wide_count * cap, loads, rank_width), bf16),
            *load_shapes,
            dma((5,)),
            dma((clusters,)),
            dma,
            dma,
            dma((wide_count, cap)),
            dma((wide_count, cap)),
            dma((narrow_count, wide_count, split)),
            dma((narrow_count, wide_count, split)),
            dma((wide_count, narrow_count)),
            dma((wide_count, narrow_count)),
        ],
        compiler_params=pltpu.CompilerParams(
            collective_id=0, has_side_effects=True, vmem_limit_bytes=60 * 1024 * 1024
        ),
    )(
        block_source.reshape(-1),
        block_cluster,
        block_rank,
        amplitudes.T,
        self_resistance,
        mode_shapes,
        in_factor.reshape(per_wide, piece_rows, rank_width),
        out_factor.reshape(per_wide, piece_rows, rank_width),
    )
    force, modal = pl.pallas_call(
        finish,
        out_shape=(
            jax.ShapeDtypeStruct(force.shape, bf16),
            jax.ShapeDtypeStruct(modal.shape, f32),
        ),
        in_specs=[vmem] * 2,
        out_specs=(vmem, vmem),
    )(force, modal)
    return force, modal.T


def solution(mesh):
    return jax.shard_map(
        per_device,
        mesh=mesh,
        in_specs=(
            P(("groups", "wide"), "narrow", None),
            P("groups", "sub"),
            P(("groups", "wide"), "narrow"),
            P(("groups", "wide"), None, "narrow", None),
            P(("groups", "wide"), None, "narrow", None),
            P("groups", None),
            P("groups"),
            P("groups"),
        ),
        out_specs=(P(("groups", "wide"), "sub", "narrow"), P(("groups", "wide", "narrow"), "sub")),
        check_vma=False,
    )
```

```python
import functools

import jax
import jax.numpy as jnp
from jax import lax
from jax.experimental import pallas as pl
from jax.experimental.pallas import tpu as pltpu
from jax.sharding import PartitionSpec as P

MESH = pl.DeviceIdType.MESH
NT = (((1,), (1,)), ((), ()))


def partner(position, step, count):
    result, bit = 0, 1
    while bit < count:
        digit = lax.rem(lax.div(position, bit), 2)
        result = result + bit * ((1 - digit) if step & bit else digit)
        bit *= 2
    return result


def slots_of(source_ref, start, per_wide, wanted, cap):
    count = jnp.int32(0)
    rows = [jnp.int32(0)] * cap
    matches, counts = [], []
    for row in range(per_wide):
        hit = source_ref[start + row] == wanted
        for slot in range(cap):
            rows[slot] = jnp.where(hit & (count == slot), row, rows[slot])
        matches.append(hit)
        counts.append(jnp.minimum(count, cap - 1))
        count = count + jnp.where(hit, 1, 0)
    return rows, matches, counts


def kernel(
    wide_count, narrow_count, cap, split, dense, scale,
    source_hbm, cluster_hbm, rank_hbm, amp_hbm, res_hbm, mode_hbm, in_hbm, out_hbm,
    force, modal_ref,
    source_ref, cluster_ref, rank_ref, amp_ref, res_ref, mode_v, in_v, out_v, vel, near, outgoing, incoming, part_own, part_send, part_recv,
    coeffs, load_send, load_own, load_recv,
    table_sem, mode_sem, in_sem, out_sem, vel_send_sem, vel_recv_sem, part_send_sem, part_recv_sem,
    load_send_sem, load_recv_sem,
):
    wide, narrow = lax.axis_index("wide"), lax.axis_index("narrow")
    clusters, piece_rows, modes = mode_v.shape
    per_wide = in_v.shape[0]
    loads = vel.shape[1]
    rank_width = in_v.shape[2]
    group = cap // split

    wides = [partner(wide, step, wide_count) for step in range(wide_count)]
    narrows = [partner(narrow, step, narrow_count) for step in range(narrow_count)]
    barrier = pltpu.get_barrier_semaphore()
    for dw in range(wide_count):
        for dn in range(narrow_count):
            if dw or dn:
                pl.semaphore_signal(
                    barrier, inc=1, device_id={"wide": wides[dw], "narrow": narrows[dn]}, device_id_type=MESH
                )

    small_copies = [
        pltpu.make_async_copy(src, dst, table_sem.at[i])
        for i, (src, dst) in enumerate(
            (
                (source_hbm, source_ref),
                (cluster_hbm, cluster_ref),
                (amp_hbm, amp_ref),
                (rank_hbm, rank_ref),
                (res_hbm, res_ref),
            )
        )
    ]
    for copy in small_copies[:3]:
        copy.start()
    mode_copies = [
        pltpu.make_async_copy(mode_hbm.at[c], mode_v.at[c], mode_sem.at[c]) for c in range(clusters)
    ]
    for copy in mode_copies:
        copy.start()
    for copy in small_copies[3:]:
        copy.start()
    in_copy = pltpu.make_async_copy(in_hbm, in_v, in_sem)
    in_copy.start()
    out_copy = pltpu.make_async_copy(out_hbm, out_v, out_sem)
    out_copy.start()

    small_copies[0].wait()
    small_copies[1].wait()
    own_start = wide * per_wide
    block_rows, slot_table = [], [jnp.int32(0)] * per_wide
    for dw in range(wide_count):
        rows, matches, counts = slots_of(source_ref, own_start, per_wide, wides[dw], cap)
        block_rows.append(rows)
        for row in range(per_wide):
            slot_table[row] = jnp.where(matches[row], dw * cap + counts[row], slot_table[row])
    wanted = []
    for dw in range(wide_count):
        rows, _, _ = slots_of(source_ref, wides[dw] * per_wide, per_wide, wide, cap)
        wanted.append([cluster_ref[wides[dw] * per_wide + row] for row in rows])

    small_copies[2].wait()
    amps = amp_ref[...]
    for c in range(clusters):
        mode_copies[c].wait()
        vel[c] = lax.dot_general(amps, mode_v[c], NT, preferred_element_type=jnp.float32).astype(jnp.bfloat16)

    pl.semaphore_wait(barrier, wide_count * narrow_count - 1)

    def vel_copy(dw, slot):
        return pltpu.make_async_remote_copy(
            src_ref=outgoing.at[dw, slot],
            dst_ref=incoming.at[dw, slot],
            send_sem=vel_send_sem.at[dw, slot],
            recv_sem=vel_recv_sem.at[dw, slot],
            device_id={"wide": wides[dw]},
            device_id_type=MESH,
        )

    def part_copy(dw, piece, dn):
        span = pl.ds(piece * group, group)
        return pltpu.make_async_remote_copy(
            src_ref=part_send.at[dw, span],
            dst_ref=part_recv.at[dn, dw, span],
            send_sem=part_send_sem.at[dn, dw, piece],
            recv_sem=part_recv_sem.at[dn, dw, piece],
            device_id={"narrow": narrows[dn]},
            device_id_type=MESH,
        )

    def load_copy(dw, dn):
        return pltpu.make_async_remote_copy(
            src_ref=load_send.at[dw, narrows[dn]],
            dst_ref=load_recv.at[dw, dn],
            send_sem=load_send_sem.at[dw, dn],
            recv_sem=load_recv_sem.at[dw, dn],
            device_id={"wide": wides[dw], "narrow": narrows[dn]},
            device_id_type=MESH,
        )

    for dw in range(1, wide_count):
        for slot in range(cap):
            outgoing[dw, slot] = vel[wanted[dw][slot]]
            vel_copy(dw, slot).start()

    for copy in small_copies[3:]:
        copy.wait()
    in_copy.wait()
    for dw in range(wide_count):
        for piece in range(split):
            for slot in range(piece * group, (piece + 1) * group):
                if dw:
                    vel_copy(dw, slot).wait_recv()
                    value = incoming[dw, slot]
                else:
                    value = vel[wanted[0][slot]]
                product = jnp.dot(value, in_v[block_rows[dw][slot]], preferred_element_type=jnp.float32)
                part_own[dw, slot] = product
                part_send[dw, slot] = product.astype(jnp.bfloat16)
            for dn in range(1, narrow_count):
                part_copy(dw, piece, dn).start()
        if dw == 0:
            for c in range(clusters):
                near[c] = (res_ref[pl.ds(c, 1), :] * vel[c].astype(jnp.float32)).astype(jnp.bfloat16)

    lanes = lax.broadcasted_iota(jnp.int32, (loads, rank_width), 1)
    for dw in range(wide_count):
        for piece in range(split):
            for dn in range(1, narrow_count):
                part_copy(dw, piece, dn).wait_recv()
            for slot in range(piece * group, (piece + 1) * group):
                total = part_own[dw, slot]
                for dn in range(1, narrow_count):
                    total = total + part_recv[dn, dw, slot].astype(jnp.float32)
                rank = rank_ref[own_start + block_rows[dw][slot]]
                coeffs[dw * cap + slot] = jnp.where(lanes < rank, total, 0.0).astype(jnp.bfloat16)

    out_copy.wait()
    blocks_per = per_wide // clusters
    for c in range(clusters):
        far = jnp.zeros((loads, piece_rows), jnp.float32)
        for k in range(blocks_per):
            row = c * blocks_per + k
            far = far + lax.dot_general(
                coeffs[slot_table[row]], out_v[row], NT, preferred_element_type=jnp.float32
            )
        far = far.astype(jnp.bfloat16).astype(jnp.float32)
        force[c] = (near[c].astype(jnp.float32) + far).astype(jnp.bfloat16)

    order = list(range(1, wide_count))[::-1] + [0]
    if dense:
        columns = modes // wide_count
        rows = columns // narrow_count
        for dw in order:
            span = pl.ds(pl.multiple_of(wides[dw] * columns, 128), columns)
            total = jnp.zeros((loads, columns), jnp.float32)
            for c in range(clusters):
                total = total + jnp.dot(force[c], mode_v[c, :, span], preferred_element_type=jnp.float32)
            total = total * scale
            for n in range(narrow_count):
                piece = total[:, n * rows : (n + 1) * rows]
                load_send[dw, n] = piece.astype(load_send.dtype)
                if dw == 0:
                    load_own[n] = piece
            for dn in range(narrow_count):
                if dw or dn:
                    load_copy(dw, dn).start()
        result = load_own[narrow]
    else:
        total = jnp.zeros((loads, modes), jnp.float32)
        for c in range(clusters):
            total = total + jnp.dot(force[c], mode_v[c], preferred_element_type=jnp.float32)
        rows = modes // (wide_count * narrow_count)
        total = (total * scale).T.reshape(wide_count, narrow_count, rows, loads)
        for w in range(wide_count):
            load_own[w] = total[w]
        for dw in order:
            load_send[dw] = load_own[wides[dw]]
            for dn in range(narrow_count):
                if dw or dn:
                    load_copy(dw, dn).start()
        result = load_own[wide, narrow]
    for dw in order:
        for dn in range(narrow_count):
            if dw or dn:
                load_copy(dw, dn).wait_recv()
                result = result + load_recv[dw, dn].astype(jnp.float32)
    modal_ref[...] = result if dense else result.T

    for dw in range(wide_count):
        if dw:
            for slot in range(cap):
                vel_copy(dw, slot).wait_send()
        for dn in range(narrow_count):
            if dn:
                for piece in range(split):
                    part_copy(dw, piece, dn).wait_send()
            if dw or dn:
                load_copy(dw, dn).wait_send()


def finish(force_ref, modal_ref, force_out, modal_out):
    force_out[...] = force_ref[...]
    modal_out[...] = modal_ref[...]


def per_device(
    mode_shapes,
    amplitudes,
    self_resistance,
    out_factor,
    in_factor,
    block_source,
    block_cluster,
    block_rank,
):
    clusters, piece_rows, modes = mode_shapes.shape
    loads = amplitudes.shape[1]
    blocks_per, rank_width = out_factor.shape[1], out_factor.shape[3]
    wide_count = lax.axis_size("wide")
    narrow_count = lax.axis_size("narrow")
    per_wide = clusters * blocks_per
    cap = min(per_wide, max(2, -(-per_wide // wide_count)))
    split = cap if wide_count <= 4 else 1
    rows = modes // (wide_count * narrow_count)
    dense = rows % 128 == 0
    scale = (modes / (wide_count * narrow_count * clusters * piece_rows)) ** 0.5
    bf16, f32 = jnp.bfloat16, jnp.float32
    if dense:
        load_shapes = [
            pltpu.VMEM((wide_count, narrow_count, loads, rows), bf16),
            pltpu.VMEM((narrow_count, loads, rows), f32),
            pltpu.VMEM((wide_count, narrow_count, loads, rows), bf16),
        ]
    else:
        load_shapes = [pltpu.VMEM((wide_count, narrow_count, rows, loads), f32)] * 3
    vmem = pl.BlockSpec(memory_space=pltpu.VMEM)
    hbm = pl.BlockSpec(memory_space=pl.ANY)
    dma = pltpu.SemaphoreType.DMA
    force, modal = pl.pallas_call(
        functools.partial(kernel, wide_count, narrow_count, cap, split, dense, scale),
        out_shape=(
            jax.ShapeDtypeStruct((clusters, loads, piece_rows), bf16),
            jax.ShapeDtypeStruct((loads, rows), f32),
        ),
        in_specs=[hbm] * 8,
        out_specs=(vmem, vmem),
        scratch_shapes=[
            pltpu.SMEM(block_cluster.shape, jnp.int32),
            pltpu.SMEM(block_cluster.shape, jnp.int32),
            pltpu.SMEM(block_cluster.shape, jnp.int32),
            pltpu.VMEM((loads, modes), bf16),
            pltpu.VMEM((clusters, piece_rows), f32),
            pltpu.VMEM((clusters, piece_rows, modes), bf16),
            pltpu.VMEM((per_wide, piece_rows, rank_width), bf16),
            pltpu.VMEM((per_wide, piece_rows, rank_width), bf16),
            pltpu.VMEM((clusters, loads, piece_rows), bf16),
            pltpu.VMEM((clusters, loads, piece_rows), bf16),
            pltpu.VMEM((wide_count, cap, loads, piece_rows), bf16),
            pltpu.VMEM((wide_count, cap, loads, piece_rows), bf16),
            pltpu.VMEM((wide_count, cap, loads, rank_width), f32),
            pltpu.VMEM((wide_count, cap, loads, rank_width), bf16),
            pltpu.VMEM((narrow_count, wide_count, cap, loads, rank_width), bf16),
            pltpu.VMEM((wide_count * cap, loads, rank_width), bf16),
            *load_shapes,
            dma((5,)),
            dma((clusters,)),
            dma,
            dma,
            dma((wide_count, cap)),
            dma((wide_count, cap)),
            dma((narrow_count, wide_count, split)),
            dma((narrow_count, wide_count, split)),
            dma((wide_count, narrow_count)),
            dma((wide_count, narrow_count)),
        ],
        compiler_params=pltpu.CompilerParams(
            collective_id=0, has_side_effects=True, vmem_limit_bytes=40 * 1024 * 1024
        ),
    )(*(pltpu.with_memory_space_constraint(operand, pltpu.HBM) for operand in (
        block_source.reshape(-1),
        block_cluster,
        block_rank,
        amplitudes.T,
        self_resistance,
        mode_shapes,
        in_factor.reshape(per_wide, piece_rows, rank_width),
        out_factor.reshape(per_wide, piece_rows, rank_width),
    )))
    force, modal = pl.pallas_call(
        finish,
        out_shape=(
            jax.ShapeDtypeStruct(force.shape, bf16),
            jax.ShapeDtypeStruct(modal.shape, f32),
        ),
        in_specs=[vmem] * 2,
        out_specs=(vmem, vmem),
        compiler_params=pltpu.CompilerParams(vmem_limit_bytes=4 * 1024 * 1024),
    )(force, modal)
    return force, modal.T


def solution(mesh):
    return jax.shard_map(
        per_device,
        mesh=mesh,
        in_specs=(
            P(("groups", "wide"), "narrow", None),
            P("groups", "sub"),
            P(("groups", "wide"), "narrow"),
            P(("groups", "wide"), None, "narrow", None),
            P(("groups", "wide"), None, "narrow", None),
            P("groups", None),
            P("groups"),
            P("groups"),
        ),
        out_specs=(P(("groups", "wide"), "sub", "narrow"), P(("groups", "wide", "narrow"), "sub")),
        check_vma=False,
    )
```
